512 devices in a mesh: ctx: 16 (over y_lo, x, core), chan: 32 (over z, y_hi).
Axes of the slice: x: 4, y: 4 (y_hi: 2, y_lo: 2; y = y_hi * 2 + y_lo), z: 16, core: 2. Of those that a mesh axis runs over, the one named last changes fastest.
Arguments:
- query_stream: bfloat16 [16384, 4096], P('ctx', 'chan'), may hold values from -6 to 6
- key_stream: bfloat16 [16384, 4096], P('ctx', 'chan'), may hold values from -6 to 6
- value_stream: bfloat16 [16384, 4096], P('ctx', 'chan'), may hold values from -6 to 6
- short_weight: float32 [3, 7, 4096], P(None, None, 'chan'), may hold values from -2 to 2
- filter_rows: float32 [256, 16384], P(None, 'chan'), may hold values from -0.046875 to 0.046875
- skip_weight: float32 [4096], P('chan'), may hold values from -4 to 4
Outputs:
- gated: bfloat16 [16384, 4096], P('ctx', 'chan')
The draws below stay inside these ranges and needn't reach their ends.
All inputs are finite; a program needn't handle non-finite values.
Results may differ from the reference program's by a relative error of at most 0.0064.
Values may be sent and summed in bfloat16 or wider, within the bound.
A program may use at most 64 MiB of HBM per device.

```python
import jax
import jax.numpy as jnp
from jax import lax

D = 4096
GROUP = 16
KSHORT = 7
SEQ = 16384
GROUPS = 256


def steps_of(rng, shape, pieces, least, top_value):
    def one(dim, shards_of):
        steps = jax.random.uniform(jax.random.fold_in(jax.random.fold_in(rng, 6), dim), (shards_of,), jnp.float32, least / len(pieces), top_value / len(pieces))
        return jnp.repeat(jnp.exp(steps), shape[dim] // shards_of).reshape((-1,) + (1,) * (len(shape) - dim - 1))

    gain = one(*pieces[0])
    for cut in pieces[1:]:
        gain = gain * one(*cut)
    return gain


def gaussian(key, dims, scale, reach, pieces=(), kind=jnp.bfloat16):
    gain = steps_of(key, dims, pieces, -0.22, 0.18) if pieces else 1.0
    array = jax.random.normal(key, dims, jnp.float32) * scale * gain
    return jnp.minimum(jnp.maximum(array, -reach), reach).astype(kind)


def setup_inputs(seed: int = 0) -> dict:
    seeds = jax.random.split(jax.random.key(seed), 7)
    return {
        "query_stream": gaussian(seeds[0], (SEQ, D), 1.0, 6.0, ((0, 16), (1, 32))),
        "key_stream": gaussian(seeds[1], (SEQ, D), 1.0, 6.0, ((0, 16), (1, 32))),
        "value_stream": gaussian(seeds[2], (SEQ, D), 1.0, 6.0, ((0, 16), (1, 32))),
        "short_weight": gaussian(seeds[3], (3, KSHORT, D), KSHORT ** -0.5, 2.0, ((2, 32),), jnp.float32),
        "filter_rows": gaussian(seeds[4], (GROUPS, SEQ), SEQ ** -0.5, 0.046875, ((1, 32),), jnp.float32),
        "skip_weight": gaussian(seeds[5], (D,), 1.0, 4.0, ((0, 32),), jnp.float32),
    }


def widen(value):
    return lax.optimization_barrier(value).astype(jnp.float32)


def causal_short(stream, tap_rows):
    length = stream.shape[0]
    padded = jnp.pad(stream.astype(jnp.float32), ((KSHORT - 1, 0), (0, 0)))
    summed = tap_rows[0] * padded[KSHORT - 1:KSHORT - 1 + length]
    for offset in range(1, KSHORT):
        summed = summed + tap_rows[offset] * padded[KSHORT - 1 - offset:KSHORT - 1 - offset + length]
    return summed


def reference(query_stream, key_stream, value_stream, short_weight, filter_rows, skip_weight):
    q_short = causal_short(query_stream, short_weight[0]).astype(jnp.bfloat16)
    product = (causal_short(key_stream, short_weight[1]) * causal_short(value_stream, short_weight[2])).astype(jnp.bfloat16)
    product_wide = widen(product)
    block_width = 128

    def one_block(block_index):
        columns = lax.dynamic_slice_in_dim(product_wide, block_index * block_width, block_width, 1)
        channel_ids = block_index * block_width + jnp.arange(block_width, dtype=jnp.int32)
        tap_block = jnp.take(filter_rows, channel_ids // GROUP, axis=0).T
        spectrum = jnp.fft.rfft(columns, n=2 * SEQ, axis=0) * jnp.fft.rfft(tap_block, n=2 * SEQ, axis=0)
        return jnp.fft.irfft(spectrum, n=2 * SEQ, axis=0)[:SEQ]

    stacked = lax.map(one_block, jnp.arange(D // block_width, dtype=jnp.int32))
    long_conv = jnp.transpose(stacked, (1, 0, 2)).reshape(SEQ, D)
    mixed = (long_conv + skip_weight[None, :] * product_wide).astype(jnp.bfloat16)
    return (widen(q_short) * widen(mixed)).astype(jnp.bfloat16)
```

```python
import functools

import jax
import jax.numpy as jnp
from jax import lax
from jax.experimental import pallas as pl
from jax.experimental.pallas import tpu as pltpu
from jax.sharding import PartitionSpec as P

GROUP = 16
KSHORT = 7
BLK = 256
LANE = 128
MESH = pl.DeviceIdType.MESH
f32 = jnp.float32
bf16 = jnp.bfloat16


def short_rows(ext, taps, stream, start, count):
    total = taps[stream, 0:1, :] * ext[stream, 16 + start:16 + start + count, :]
    for j in range(1, KSHORT):
        total = total + taps[stream, j:j + 1, :] * ext[stream, 16 + start - j:16 + start - j + count, :]
    return total


def build_toeplitz(taps128, tiles, count):
    row = lax.broadcasted_iota(jnp.int32, (LANE, LANE), 0)
    col = lax.broadcasted_iota(jnp.int32, (LANE, LANE), 1)
    keep = col >= row
    tiles[0] = jnp.zeros((LANE, LANE), bf16)

    def turned(r):
        line = jnp.broadcast_to(taps128[r], (LANE, LANE))
        return pltpu.roll(line, 0, 1, stride=1, stride_axis=0)

    def body(r, before):
        now = turned(r)
        tiles[r + 1] = jnp.where(keep, now, before).astype(bf16)
        return now

    lax.fori_loop(0, count, body, jnp.zeros((LANE, LANE), f32))


def long_conv(xcat, tiles, acc, depth):
    rows = acc.shape[0]
    step = 8 * depth
    for e in range(rows // step):
        parts = []
        for q in range(depth):
            d = e * depth + q
            parts.append(jnp.concatenate([tiles[2 * d + 1], tiles[2 * d + 2]], axis=1))
            parts.append(jnp.concatenate([tiles[2 * d], tiles[2 * d + 1]], axis=1))
        weights = jnp.concatenate(parts, axis=0)
        part = jnp.dot(xcat[0:rows - step * e, :], weights, preferred_element_type=f32)
        if e == 0:
            acc[...] = part
        else:
            acc[step * e:rows, :] += part


DEPTH = 8


def kernel(n_ctx, n_chan, q_hbm, k_hbm, v_hbm, taps_hbm, filt_hbm, skip_hbm, out_hbm,
           raw, taps, filt, skip, ext, halo, qshort, prod, fsend, fgot, xsend, xgot, skipc, xpad, xcat, tiles, acc,
           osend, ogot, outv,
           load_sem, h_send, h_recv, f_send, f_recv, x_send, x_recv, o_send, o_recv):
    me = lax.axis_index("ctx")
    ch = lax.axis_index("chan")
    rows, width = raw.shape[1], raw.shape[2]
    blocks = rows // BLK

    streams = (q_hbm, k_hbm, v_hbm)
    loads = [pltpu.make_async_copy(streams[s], raw.at[s], load_sem.at[s]) for s in range(3)]
    loads.append(pltpu.make_async_copy(taps_hbm, taps, load_sem.at[3]))
    loads.append(pltpu.make_async_copy(skip_hbm, skip, load_sem.at[4]))
    pieces = filt.shape[0]
    for p in range(pieces):
        loads.append(pltpu.make_async_copy(filt_hbm.at[:, LANE * p:LANE * (p + 1)], filt.at[p], load_sem.at[5 + p]))
    for load in loads:
        load.start()

    barrier = pltpu.get_barrier_semaphore()

    def greet_ctx(k, _):
        pl.semaphore_signal(barrier, inc=1, device_id=(lax.rem(me + k, n_ctx), ch), device_id_type=MESH)
        return 0

    def greet_chan(k, _):
        pl.semaphore_signal(barrier, inc=1, device_id=(me, lax.rem(ch + k, n_chan)), device_id_type=MESH)
        return 0

    lax.fori_loop(1, n_chan, greet_chan, 0)
    lax.fori_loop(1, n_ctx, greet_ctx, 0)

    for load in loads:
        load.wait()

    for p in range(pieces):
        fsend[:, p, :] = filt[p, pl.ds(me // 2, n_chan, stride=8), :]

    for s in range(3):
        ext[s, 0:16, :] = jnp.zeros((16, width), f32)
        ext[s, 16:16 + rows, :] = raw[s].astype(f32)
    qshort[...] = short_rows(ext, taps, 0, 0, rows)
    prod[...] = short_rows(ext, taps, 1, 0, rows) * short_rows(ext, taps, 2, 0, rows)
    skipc[...] = jnp.broadcast_to(skip[...], (width, width)).T

    def lay_out(pair):
        both = []
        for i in (2 * pair, 2 * pair + 1):
            both.append(prod[BLK * i:BLK * (i + 1), :].T.reshape(n_ctx, 8, BLK))
        xsend[pair] = jnp.concatenate(both, axis=1).astype(bf16)

    lay_out(1)

    pl.semaphore_wait(barrier, n_ctx - 1 + n_chan - 1)

    @pl.when(me < n_ctx - 1)
    def _():
        for s in range(3):
            pltpu.make_async_remote_copy(raw.at[s, rows - 16:rows], halo.at[s], h_send.at[s], h_recv.at[s],
                                         device_id=(me + 1, ch), device_id_type=MESH).start()

    def filter_copy(to, slot):
        return pltpu.make_async_remote_copy(fsend.at[to], fgot.at[slot], f_send.at[to], f_recv.at[slot],
                                            device_id=(me, to), device_id_type=MESH)

    def send_filter(k, _):
        filter_copy(lax.rem(ch + k, n_chan), ch).start()
        return 0

    lax.fori_loop(1, n_chan, send_filter, 0)
    fgot[ch] = fsend[ch]

    def block_copy(pair, to, slot):
        return pltpu.make_async_remote_copy(xsend.at[pair, to], xgot.at[pair, slot], x_send.at[pair, to],
                                            x_recv.at[pair, slot], device_id=(to, ch), device_id_type=MESH)

    def send_blocks(pair):
        def body(k, _):
            block_copy(pair, lax.rem(me + k, n_ctx), me).start()
            return 0

        lax.fori_loop(1, n_ctx, body, 0)
        xgot[pair, me] = xsend[pair, me]

    send_blocks(1)

    @pl.when(me > 0)
    def _():
        for s in range(3):
            pltpu.make_async_remote_copy(raw.at[s, rows - 16:rows], halo.at[s], h_send.at[s], h_recv.at[s],
                                         device_id=(me - 1, ch), device_id_type=MESH).wait_recv()
            ext[s, 0:16, :] = halo[s].astype(f32)
        qshort[0:8, :] = short_rows(ext, taps, 0, 0, 8)
        prod[0:8, :] = short_rows(ext, taps, 1, 0, 8) * short_rows(ext, taps, 2, 0, 8)

    lay_out(0)
    send_blocks(0)

    def wait_blocks(pair):
        def body(k, _):
            block_copy(pair, lax.rem(me + k, n_ctx), lax.rem(me + k, n_ctx)).wait_recv()
            return 0

        lax.fori_loop(1, n_ctx, body, 0)

    wait_blocks(1)
    wait_blocks(0)

    xpad[0:8 * DEPTH, :] = jnp.zeros((8 * DEPTH, BLK), f32)
    for source in range(n_ctx):
        for pair in range(2):
            start = 8 * DEPTH + 8 * (source * blocks + 2 * pair)
            xpad[start:start + 16, :] = xgot[pair, source].astype(f32)
    total_rows = acc.shape[0]
    for q in range(DEPTH):
        xcat[:, BLK * q:BLK * (q + 1)] = xpad[8 * (DEPTH - q):8 * (DEPTH - q) + total_rows, :].astype(bf16)

    def wait_filter(k, _):
        filter_copy(lax.rem(ch + k, n_chan), lax.rem(ch + k, n_chan)).wait_recv()
        return 0

    lax.fori_loop(1, n_chan, wait_filter, 0)

    class Taps:
        def __getitem__(self, r):
            return fgot[r // 4, pl.ds(lax.rem(r, 4), 1), :]

    build_toeplitz(Taps(), tiles, 4 * n_chan)
    long_conv(xcat, tiles, acc, DEPTH)

    own = skipc[pl.ds(pl.multiple_of(me * 8, 8), 8), :]
    own = jnp.concatenate([own, own], axis=1)
    for dest in range(n_ctx):
        part = acc[dest * 8 * blocks:(dest + 1) * 8 * blocks, :].reshape(blocks, 8, BLK)
        start = 8 * DEPTH + dest * 8 * blocks
        signal = xpad[start:start + 8 * blocks, :].reshape(blocks, 8, BLK)
        osend[dest] = (part + own[None] * signal).astype(bf16).reshape(8 * blocks, BLK)

    def mixed_copy(to, slot):
        return pltpu.make_async_remote_copy(osend.at[to], ogot.at[slot], o_send.at[to], o_recv.at[slot],
                                            device_id=(to, ch), device_id_type=MESH)

    def send_mixed(k, _):
        mixed_copy(lax.rem(me + k, n_ctx), me).start()
        return 0

    lax.fori_loop(1, n_ctx, send_mixed, 0)
    ogot[me] = osend[me]

    def wait_mixed(k, _):
        mixed_copy(lax.rem(me + k, n_ctx), lax.rem(me + k, n_ctx)).wait_recv()
        return 0

    lax.fori_loop(1, n_ctx, wait_mixed, 0)

    wide = ogot[...].astype(f32)
    for i in range(blocks):
        piece = wide[:, 8 * i:8 * (i + 1), :].reshape(width, BLK).T
        rounded = qshort[BLK * i:BLK * (i + 1), :].astype(bf16).astype(f32)
        outv[BLK * i:BLK * (i + 1), :] = (rounded * piece).astype(bf16)
    store = pltpu.make_async_copy(outv, out_hbm, load_sem.at[0])
    store.start()

    @pl.when(me < n_ctx - 1)
    def _():
        for s in range(3):
            pltpu.make_async_remote_copy(raw.at[s, rows - 16:rows], halo.at[s], h_send.at[s], h_recv.at[s],
                                         device_id=(me + 1, ch), device_id_type=MESH).wait_send()

    def end_filter(k, _):
        filter_copy(lax.rem(ch + k, n_chan), ch).wait_send()
        return 0

    lax.fori_loop(1, n_chan, end_filter, 0)

    def end_blocks(k, _):
        to = lax.rem(me + k, n_ctx)
        block_copy(0, to, me).wait_send()
        block_copy(1, to, me).wait_send()
        mixed_copy(to, me).wait_send()
        return 0

    lax.fori_loop(1, n_ctx, end_blocks, 0)
    store.wait()


def local(mesh_shape, query_stream, key_stream, value_stream, short_weight, filter_rows, skip_weight):
    n_ctx, n_chan = mesh_shape
    rows, width = query_stream.shape
    piece = filter_rows.shape[1]
    total = rows * n_ctx // BLK * 8
    dma = pltpu.SemaphoreType.DMA
    return pl.pallas_call(
        functools.partial(kernel, n_ctx, n_chan),
        out_shape=jax.ShapeDtypeStruct((rows, width), bf16),
        in_specs=[pl.BlockSpec(memory_space=pl.ANY)] * 6,
        out_specs=pl.BlockSpec(memory_space=pl.ANY),
        scratch_shapes=[
            pltpu.VMEM((3, rows, width), bf16),
            pltpu.VMEM(short_weight.shape, f32),
            pltpu.VMEM((piece // LANE, filter_rows.shape[0], LANE), f32),
            pltpu.VMEM((1, width), f32),
            pltpu.VMEM((3, rows + 16, width), f32),
            pltpu.VMEM((3, 16, width), bf16),
            pltpu.VMEM((rows, width), f32),
            pltpu.VMEM((rows, width), f32),
            pltpu.VMEM((n_chan, piece // LANE, LANE), f32),
            pltpu.VMEM((n_chan, piece // LANE, LANE), f32),
            pltpu.VMEM((2, n_ctx, 16, BLK), bf16),
            pltpu.VMEM((2, n_ctx, 16, BLK), bf16),
            pltpu.VMEM((width, width), f32),
            pltpu.VMEM((total + 8 * DEPTH, BLK), f32),
            pltpu.VMEM((total, DEPTH * BLK), bf16),
            pltpu.VMEM((n_chan * piece // LANE + 1, LANE, LANE), bf16),
            pltpu.VMEM((total, BLK), f32),
            pltpu.VMEM((n_ctx, total // n_ctx, BLK), bf16),
            pltpu.VMEM((n_ctx, total // n_ctx, BLK), bf16),
            pltpu.VMEM((rows, width), bf16),
            dma((5 + piece // LANE,)),
            dma((3,)), dma((3,)),
            dma((n_chan,)), dma((n_chan,)),
            dma((2, n_ctx)), dma((2, n_ctx)),
            dma((n_ctx,)), dma((n_ctx,)),
        ],
        compiler_params=pltpu.CompilerParams(collective_id=0, has_side_effects=True, vmem_limit_bytes=48 * 1024 * 1024),
    )(query_stream, key_stream, value_stream, short_weight, filter_rows, skip_weight.reshape(1, width))


def solution(mesh):
    return jax.shard_map(
        functools.partial(local, (mesh.shape["ctx"], mesh.shape["chan"])),
        mesh=mesh,
        in_specs=(
            P("ctx", "chan"),
            P("ctx", "chan"),
            P("ctx", "chan"),
            P(None, None, "chan"),
            P(None, "chan"),
            P("chan"),
        ),
        out_specs=P("ctx", "chan"),
        check_vma=False,
    )
```

```python
import functools

import jax
import jax.numpy as jnp
from jax import lax
from jax.experimental import pallas as pl
from jax.experimental.pallas import tpu as pltpu
from jax.sharding import PartitionSpec as P

GROUP = 16
KSHORT = 7
BLK = 256
LANE = 128
MESH = pl.DeviceIdType.MESH
f32 = jnp.float32
bf16 = jnp.bfloat16


def short_rows(ext, taps, stream, start, count):
    total = taps[stream, 0:1, :] * ext[stream, 16 + start:16 + start + count, :]
    for j in range(1, KSHORT):
        total = total + taps[stream, j:j + 1, :] * ext[stream, 16 + start - j:16 + start - j + count, :]
    return total


UNIT = 8
SHIFTS = UNIT // 2 + 1


def unit_tiles(lines, tiles):
    row = lax.broadcasted_iota(jnp.int32, (LANE, LANE), 0)
    col = lax.broadcasted_iota(jnp.int32, (LANE, LANE), 1)
    keep = col >= row
    zero = jnp.zeros((LANE, LANE), f32)
    firsts = [pltpu.roll(jnp.broadcast_to(line, (8, LANE)), 0, 1, stride=1, stride_axis=0) for line in lines]
    before = zero
    for r in range(UNIT + 1):
        now = zero
        if r < UNIT:
            now = jnp.concatenate([firsts[r]] + [pltpu.roll(firsts[r], 8 * k, 1) for k in range(1, LANE // 8)], axis=0)
        tiles[r + 1] = jnp.where(keep, now, before).astype(bf16)
        before = now


def unit_conv(xcat, tiles, acc, start, rows):
    parts = []
    for q in range(SHIFTS):
        parts.append(jnp.concatenate([tiles[2 * q + 1], tiles[2 * q + 2]], axis=1))
        parts.append(jnp.concatenate([tiles[2 * q], tiles[2 * q + 1]], axis=1))
    weights = jnp.concatenate(parts, axis=0)
    acc[pl.ds(start, rows), :] += jnp.dot(xcat[0:rows, :], weights, preferred_element_type=f32)


def kernel(n_ctx, n_chan, q_hbm, k_hbm, v_hbm, taps_hbm, filt_hbm, skip_hbm, out_hbm,
           raw, taps, filt, skip, ext, halo, qshort, prod, fsend, fgot, xsend, xgot, skipc, xpad, xcat, tiles, acc,
           osend, ogot, outv,
           load_sem, ready, h_send, h_recv, f_send, f_recv, x_send, x_recv, o_send, o_recv):
    me = lax.axis_index("ctx")
    ch = lax.axis_index("chan")
    rows, width = raw.shape[1], raw.shape[2]
    blocks = rows // BLK

    streams = (q_hbm, k_hbm, v_hbm)
    loads = [pltpu.make_async_copy(streams[s], raw.at[s], load_sem.at[s]) for s in range(3)]
    loads.append(pltpu.make_async_copy(taps_hbm, taps, load_sem.at[3]))
    loads.append(pltpu.make_async_copy(skip_hbm, skip, load_sem.at[4]))
    pieces = filt.shape[0]
    for p in range(pieces):
        loads.append(pltpu.make_async_copy(filt_hbm.at[:, LANE * p:LANE * (p + 1)], filt.at[p], load_sem.at[5 + p]))
    for load in loads:
        load.start()

    barrier = pltpu.get_barrier_semaphore()

    def greet_ctx(k, _):
        pl.semaphore_signal(barrier, inc=1, device_id=(lax.rem(me + k, n_ctx), ch), device_id_type=MESH)
        return 0

    def greet_chan(to, _):
        pl.semaphore_signal(barrier, inc=1, device_id=(me, to), device_id_type=MESH)
        return 0

    lax.fori_loop(1, n_ctx, greet_ctx, 0)
    lax.fori_loop(ch + 1, n_chan, greet_chan, 0)

    for load in loads:
        load.wait()

    for p in range(pieces):
        fsend[:, p, :] = filt[p, pl.ds(me // 2, n_chan, stride=8), :]

    for s in range(3):
        ext[s, 0:16, :] = jnp.zeros((16, width), f32)
        ext[s, 16:16 + rows, :] = raw[s].astype(f32)
    qshort[...] = short_rows(ext, taps, 0, 0, rows)
    prod[...] = short_rows(ext, taps, 1, 0, rows) * short_rows(ext, taps, 2, 0, rows)
    skipc[...] = jnp.broadcast_to(skip[...], (width, width)).T

    def lay_out(pair):
        both = []
        for i in (2 * pair, 2 * pair + 1):
            both.append(prod[BLK * i:BLK * (i + 1), :].T.reshape(n_ctx, 8, BLK))
        xsend[pair] = jnp.concatenate(both, axis=1).astype(bf16)

    lay_out(1)

    pl.semaphore_wait(barrier, n_ctx - 1 + ch)

    @pl.when(me < n_ctx - 1)
    def _():
        for s in range(3):
            pltpu.make_async_remote_copy(raw.at[s, rows - 16:rows], halo.at[s], h_send.at[s], h_recv.at[s],
                                         device_id=(me + 1, ch), device_id_type=MESH).start()

    def filter_copy(to, slot):
        return pltpu.make_async_remote_copy(fsend.at[to], fgot.at[slot], f_send.at[to], f_recv.at[slot],
                                            device_id=(me, to), device_id_type=MESH)

    def send_back(k, _):
        to = ch - k
        filter_copy(to, ch).start()
        pl.semaphore_signal(ready.at[ch], inc=1, device_id=(me, to), device_id_type=MESH)
        return 0

    lax.fori_loop(1, ch + 1, send_back, 0)
    fgot[ch] = fsend[ch]

    def block_copy(pair, to, slot):
        return pltpu.make_async_remote_copy(xsend.at[pair, to], xgot.at[pair, slot], x_send.at[pair, to],
                                            x_recv.at[pair, slot], device_id=(to, ch), device_id_type=MESH)

    def send_blocks(pair):
        def body(k, _):
            block_copy(pair, lax.rem(me + k, n_ctx), me).start()
            return 0

        lax.fori_loop(1, n_ctx, body, 0)
        xgot[pair, me] = xsend[pair, me]

    send_blocks(1)

    @pl.when(me > 0)
    def _():
        for s in range(3):
            pltpu.make_async_remote_copy(raw.at[s, rows - 16:rows], halo.at[s], h_send.at[s], h_recv.at[s],
                                         device_id=(me - 1, ch), device_id_type=MESH).wait_recv()
            ext[s, 0:16, :] = halo[s].astype(f32)
        qshort[0:8, :] = short_rows(ext, taps, 0, 0, 8)
        prod[0:8, :] = short_rows(ext, taps, 1, 0, 8) * short_rows(ext, taps, 2, 0, 8)

    lay_out(0)
    send_blocks(0)

    def wait_blocks(pair):
        def body(k, _):
            block_copy(pair, lax.rem(me + k, n_ctx), lax.rem(me + k, n_ctx)).wait_recv()
            return 0

        lax.fori_loop(1, n_ctx, body, 0)

    wait_blocks(1)
    wait_blocks(0)

    xpad[0:8 * SHIFTS, :] = jnp.zeros((8 * SHIFTS, BLK), f32)
    for source in range(n_ctx):
        for pair in range(2):
            start = 8 * SHIFTS + 8 * (source * blocks + 2 * pair)
            xpad[start:start + 16, :] = xgot[pair, source].astype(f32)
    for q in range(SHIFTS):
        xcat[:, BLK * q:BLK * (q + 1)] = xpad[8 * (SHIFTS - q):8 * (SHIFTS - q) + xcat.shape[0], :].astype(bf16)
    acc[...] = jnp.zeros_like(acc)

    n_unit = n_chan // 2
    mine = ch // 2

    def unit_at(s):
        low = jnp.where(s > 2 * mine, s, jnp.where(s % 2 == 1, mine + (s + 1) // 2, mine - s // 2))
        step = jnp.where(s % 2 == 1, n_unit - (s + 1) // 2, s // 2)
        high = lax.rem(mine + step, n_unit)
        return jnp.where(mine < n_unit // 2, low, high)

    def forward(unit):
        for y in range(2):
            to = 2 * unit + y

            @pl.when(to > ch)
            def _():
                pl.semaphore_wait(ready.at[to], 1)
                filter_copy(to, ch).start()

    def add_unit(s, _):
        unit = unit_at(s)

        @pl.when(s < n_unit - 1)
        def _():
            forward(unit_at(s + 1))

        for y in range(2):
            source = 2 * unit + y

            @pl.when(source != ch)
            def _():
                filter_copy(source, source).wait_recv()

        taps_of = [fgot[2 * unit + r // 4, r % 4:r % 4 + 1, :] for r in range(UNIT)]
        unit_tiles(taps_of, tiles)
        span = 8 * UNIT // 2
        quarter = n_unit // 4
        for part in range(4):
            @pl.when(unit // quarter == part)
            def _():
                unit_conv(xcat, tiles, acc, pl.multiple_of(span * unit, span), xcat.shape[0] - span * quarter * part)
        return 0

    tiles[0] = jnp.zeros((LANE, LANE), bf16)
    tiles[UNIT + 2] = jnp.zeros((LANE, LANE), bf16)
    forward(mine)
    lax.fori_loop(0, n_unit, add_unit, 0)

    own = skipc[pl.ds(pl.multiple_of(me * 8, 8), 8), :]
    own = jnp.concatenate([own, own], axis=1)
    for dest in range(n_ctx):
        part = acc[dest * 8 * blocks:(dest + 1) * 8 * blocks, :].reshape(blocks, 8, BLK)
        start = 8 * SHIFTS + dest * 8 * blocks
        signal = xpad[start:start + 8 * blocks, :].reshape(blocks, 8, BLK)
        osend[dest] = (part + own[None] * signal).astype(bf16).reshape(8 * blocks, BLK)

    def mixed_copy(to, slot):
        return pltpu.make_async_remote_copy(osend.at[to], ogot.at[slot], o_send.at[to], o_recv.at[slot],
                                            device_id=(to, ch), device_id_type=MESH)

    def send_mixed(k, _):
        mixed_copy(lax.rem(me + k, n_ctx), me).start()
        return 0

    lax.fori_loop(1, n_ctx, send_mixed, 0)
    ogot[me] = osend[me]

    def wait_mixed(k, _):
        mixed_copy(lax.rem(me + k, n_ctx), lax.rem(me + k, n_ctx)).wait_recv()
        return 0

    lax.fori_loop(1, n_ctx, wait_mixed, 0)

    wide = ogot[...].astype(f32)
    for i in range(blocks):
        piece = wide[:, 8 * i:8 * (i + 1), :].reshape(width, BLK).T
        rounded = qshort[BLK * i:BLK * (i + 1), :].astype(bf16).astype(f32)
        outv[BLK * i:BLK * (i + 1), :] = (rounded * piece).astype(bf16)
    store = pltpu.make_async_copy(outv, out_hbm, load_sem.at[0])
    store.start()

    @pl.when(me < n_ctx - 1)
    def _():
        for s in range(3):
            pltpu.make_async_remote_copy(raw.at[s, rows - 16:rows], halo.at[s], h_send.at[s], h_recv.at[s],
                                         device_id=(me + 1, ch), device_id_type=MESH).wait_send()

    def end_filter(k, _):
        filter_copy(lax.rem(ch + k, n_chan), ch).wait_send()
        return 0

    lax.fori_loop(1, n_chan, end_filter, 0)

    def end_blocks(k, _):
        to = lax.rem(me + k, n_ctx)
        block_copy(0, to, me).wait_send()
        block_copy(1, to, me).wait_send()
        mixed_copy(to, me).wait_send()
        return 0

    lax.fori_loop(1, n_ctx, end_blocks, 0)
    store.wait()


def local(mesh_shape, query_stream, key_stream, value_stream, short_weight, filter_rows, skip_weight):
    n_ctx, n_chan = mesh_shape
    rows, width = query_stream.shape
    piece = filter_rows.shape[1]
    total = rows * n_ctx // BLK * 8
    dma = pltpu.SemaphoreType.DMA
    return pl.pallas_call(
        functools.partial(kernel, n_ctx, n_chan),
        out_shape=jax.ShapeDtypeStruct((rows, width), bf16),
        in_specs=[pl.BlockSpec(memory_space=pltpu.HBM)] * 6,
        out_specs=pl.BlockSpec(memory_space=pl.ANY),
        scratch_shapes=[
            pltpu.VMEM((3, rows, width), bf16),
            pltpu.VMEM(short_weight.shape, f32),
            pltpu.VMEM((piece // LANE, filter_rows.shape[0], LANE), f32),
            pltpu.VMEM((1, width), f32),
            pltpu.VMEM((3, rows + 16, width), f32),
            pltpu.VMEM((3, 16, width), bf16),
            pltpu.VMEM((rows, width), f32),
            pltpu.VMEM((rows, width), f32),
            pltpu.VMEM((n_chan, piece // LANE, LANE), f32),
            pltpu.VMEM((n_chan, piece // LANE, LANE), f32),
            pltpu.VMEM((2, n_ctx, 16, BLK), bf16),
            pltpu.VMEM((2, n_ctx, 16, BLK), bf16),
            pltpu.VMEM((width, width), f32),
            pltpu.VMEM((total + 8 * SHIFTS, BLK), f32),
            pltpu.VMEM((total, SHIFTS * BLK), bf16),
            pltpu.VMEM((UNIT + 3, LANE, LANE), bf16),
            pltpu.VMEM((total + total // 2, BLK), f32),
            pltpu.VMEM((n_ctx, total // n_ctx, BLK), bf16),
            pltpu.VMEM((n_ctx, total // n_ctx, BLK), bf16),
            pltpu.VMEM((rows, width), bf16),
            dma((5 + piece // LANE,)),
            pltpu.SemaphoreType.REGULAR((n_chan,)),
            dma((3,)), dma((3,)),
            dma((n_chan,)), dma((n_chan,)),
            dma((2, n_ctx)), dma((2, n_ctx)),
            dma((n_ctx,)), dma((n_ctx,)),
        ],
        compiler_params=pltpu.CompilerParams(collective_id=0, has_side_effects=True, vmem_limit_bytes=63 * 1024 * 1024),
    )(query_stream, key_stream, value_stream, short_weight, filter_rows, skip_weight.reshape(1, width))


def solution(mesh):
    return jax.shard_map(
        functools.partial(local, (mesh.shape["ctx"], mesh.shape["chan"])),
        mesh=mesh,
        in_specs=(
            P("ctx", "chan"),
            P("ctx", "chan"),
            P("ctx", "chan"),
            P(None, None, "chan"),
            P(None, "chan"),
            P("chan"),
        ),
        out_specs=P("ctx", "chan"),
        check_vma=False,
    )
```

```python
import functools

import jax
import jax.numpy as jnp
from jax import lax
from jax.experimental import pallas as pl
from jax.experimental.pallas import tpu as pltpu
from jax.sharding import PartitionSpec as P

GROUP = 16
KSHORT = 7
BLK = 256
LANE = 128
MESH = pl.DeviceIdType.MESH
f32 = jnp.float32
bf16 = jnp.bfloat16


def short_rows(ext, taps, stream, start, count):
    total = taps[stream, 0:1, :] * ext[stream, 16 + start:16 + start + count, :]
    for j in range(1, KSHORT):
        total = total + taps[stream, j:j + 1, :] * ext[stream, 16 + start - j:16 + start - j + count, :]
    return total


UNIT = 8
DEPTH = 8


def unit_tiles(lines, tiles, lower, unit):
    row = lax.broadcasted_iota(jnp.int32, (LANE, LANE), 0)
    col = lax.broadcasted_iota(jnp.int32, (LANE, LANE), 1)
    keep = col >= row
    zero = jnp.zeros((LANE, LANE), f32)
    firsts = [pltpu.roll(jnp.broadcast_to(line, (8, LANE)), 0, 1, stride=1, stride_axis=0) for line in lines]
    before = zero
    for r in range(UNIT):
        now = jnp.concatenate([firsts[r]] + [pltpu.roll(firsts[r], 8 * k, 1) for k in range(1, LANE // 8)], axis=0)
        tiles[UNIT * unit + r + 1] = jnp.where(keep, now, before).astype(bf16)
        before = now
    lower[unit] = jnp.where(keep, zero, before).astype(bf16)


def join_units(tiles, lower, units):
    for unit in range(1, units):
        tiles[UNIT * unit + 1] = tiles[UNIT * unit + 1] + lower[unit - 1]
    tiles[UNIT * units + 1] = lower[units - 1]


def half_conv(xcat, tiles, acc, which, depths):
    total = xcat.shape[0]
    first = which * 8 * depths
    for e in range(depths // DEPTH):
        parts = []
        for q in range(DEPTH):
            d = e * DEPTH + q
            parts.append(jnp.concatenate([tiles[2 * d + 1], tiles[2 * d + 2]], axis=1))
            parts.append(jnp.concatenate([tiles[2 * d], tiles[2 * d + 1]], axis=1))
        start = first + 8 * DEPTH * e
        acc[start:total, :] += jnp.dot(xcat[0:total - start, :], jnp.concatenate(parts, axis=0), preferred_element_type=f32)
    start = first + 8 * depths
    if start < total:
        d = depths
        weights = jnp.concatenate([jnp.concatenate([tiles[2 * d + 1], tiles[2 * d + 2]], axis=1),
                                   jnp.concatenate([tiles[2 * d], tiles[2 * d + 1]], axis=1)], axis=0)
        acc[start:total, :] += jnp.dot(xcat[0:total - start, 0:BLK], weights, preferred_element_type=f32)


def kernel(n_ctx, n_chan, q_hbm, k_hbm, v_hbm, taps_hbm, filt_hbm, skip_hbm, out_hbm,
           raw, taps, filt, skip, ext, halo, qshort, prod, fsend, fgot, xsend, xgot, skipc, xpad, xcat, tiles, lower, acc,
           osend, ogot, outv,
           load_sem, ready, h_send, h_recv, f_send, f_recv, x_send, x_recv, o_send, o_recv):
    me = lax.axis_index("ctx")
    ch = lax.axis_index("chan")
    rows, width = raw.shape[1], raw.shape[2]
    blocks = rows // BLK

    streams = (q_hbm, k_hbm, v_hbm)
    loads = [pltpu.make_async_copy(streams[s], raw.at[s], load_sem.at[s]) for s in range(3)]
    loads.append(pltpu.make_async_copy(taps_hbm, taps, load_sem.at[3]))
    loads.append(pltpu.make_async_copy(skip_hbm, skip, load_sem.at[4]))
    pieces = filt.shape[0]
    for p in range(pieces):
        loads.append(pltpu.make_async_copy(filt_hbm.at[:, LANE * p:LANE * (p + 1)], filt.at[p], load_sem.at[5 + p]))
    for load in loads:
        load.start()

    barrier = pltpu.get_barrier_semaphore()

    def greet_ctx(k, _):
        pl.semaphore_signal(barrier, inc=1, device_id=(lax.rem(me + k, n_ctx), ch), device_id_type=MESH)
        return 0

    def greet_chan(to, _):
        pl.semaphore_signal(barrier, inc=1, device_id=(me, to), device_id_type=MESH)
        return 0

    lax.fori_loop(1, n_ctx, greet_ctx, 0)
    lax.fori_loop(ch + 1, n_chan, greet_chan, 0)

    for load in loads:
        load.wait()

    for p in range(pieces):
        fsend[:, p, :] = filt[p, pl.ds(me // 2, n_chan, stride=8), :]

    def lay_out(pair):
        both = []
        for i in (2 * pair, 2 * pair + 1):
            both.append(prod[BLK * i:BLK * (i + 1), :].T.reshape(n_ctx, 8, BLK))
        xsend[pair] = jnp.concatenate(both, axis=1).astype(bf16)

    skipc[...] = jnp.broadcast_to(skip[...], (width, width)).T
    acc[...] = jnp.zeros_like(acc)
    tiles[0] = jnp.zeros((LANE, LANE), bf16)
    tiles[tiles.shape[0] - 1] = jnp.zeros((LANE, LANE), bf16)

    pl.semaphore_wait(barrier, n_ctx - 1 + ch)

    @pl.when(me < n_ctx - 1)
    def _():
        for s in range(3):
            pltpu.make_async_remote_copy(raw.at[s, rows - 16:rows], halo.at[s], h_send.at[s], h_recv.at[s],
                                         device_id=(me + 1, ch), device_id_type=MESH).start()

    def filter_copy(to, slot):
        return pltpu.make_async_remote_copy(fsend.at[to], fgot.at[slot], f_send.at[to], f_recv.at[slot],
                                            device_id=(me, to), device_id_type=MESH)

    def send_back(k, _):
        to = ch - k
        filter_copy(to, ch).start()
        pl.semaphore_signal(ready.at[ch], inc=1, device_id=(me, to), device_id_type=MESH)
        return 0

    lax.fori_loop(1, ch + 1, send_back, 0)
    fgot[ch] = fsend[ch]

    def block_copy(pair, to, slot):
        return pltpu.make_async_remote_copy(xsend.at[pair, to], xgot.at[pair, slot], x_send.at[pair, to],
                                            x_recv.at[pair, slot], device_id=(to, ch), device_id_type=MESH)

    def send_blocks(pair):
        def body(k, _):
            block_copy(pair, lax.rem(me + k, n_ctx), me).start()
            return 0

        lax.fori_loop(1, n_ctx, body, 0)
        xgot[pair, me] = xsend[pair, me]

    for s in range(3):
        ext[s, 0:16, :] = jnp.zeros((16, width), f32)
        ext[s, 16:16 + rows, :] = raw[s].astype(f32)
    prod[...] = short_rows(ext, taps, 1, 0, rows) * short_rows(ext, taps, 2, 0, rows)
    lay_out(1)
    send_blocks(1)

    @pl.when(me > 0)
    def _():
        for s in range(3):
            pltpu.make_async_remote_copy(raw.at[s, rows - 16:rows], halo.at[s], h_send.at[s], h_recv.at[s],
                                         device_id=(me - 1, ch), device_id_type=MESH).wait_recv()
            ext[s, 0:16, :] = halo[s].astype(f32)
        prod[0:8, :] = short_rows(ext, taps, 1, 0, 8) * short_rows(ext, taps, 2, 0, 8)

    lay_out(0)
    send_blocks(0)
    qshort[...] = short_rows(ext, taps, 0, 0, rows)

    n_unit = n_chan // 2
    half = n_unit // 2
    mine = ch // 2
    place = lax.rem(mine, half)
    base = mine - place
    early = mine < half

    def unit_at(s):
        turn = jnp.where(s < half, s, n_unit - 1 - s)
        swing = jnp.where(turn % 2 == 1, place + (turn + 1) // 2, place - turn // 2)
        rest = jnp.where(place < half // 2, turn, half - 1 - turn)
        local_unit = jnp.where(turn <= 2 * jnp.minimum(place, half - 1 - place), swing, rest)
        return jnp.where(s < half, base, half - base) + local_unit

    def answer(s, _):
        for y in range(2):
            to = 2 * unit_at(s) + y

            @pl.when(to > ch)
            def _():
                pl.semaphore_wait(ready.at[to], 1)
                filter_copy(to, ch).start()
        return 0

    def take_unit(s, _):
        unit = unit_at(s)

        @pl.when(s + 1 < half)
        def _():
            answer(s + 1, 0)

        for y in range(2):
            source = 2 * unit + y

            @pl.when(source != ch)
            def _():
                filter_copy(source, source).wait_recv()

        unit_tiles([fgot[2 * unit + r // 4, r % 4:r % 4 + 1, :] for r in range(UNIT)], tiles, lower, lax.rem(unit, half))
        return 0

    def wait_blocks(pair):
        def body(k, _):
            block_copy(pair, lax.rem(me + k, n_ctx), lax.rem(me + k, n_ctx)).wait_recv()
            return 0

        lax.fori_loop(1, n_ctx, body, 0)

    def mixed_copy(to, slot):
        return pltpu.make_async_remote_copy(osend.at[to], ogot.at[slot], o_send.at[to], o_recv.at[slot],
                                            device_id=(to, ch), device_id_type=MESH)

    own = skipc[pl.ds(pl.multiple_of(me * 8, 8), 8), :]
    own = jnp.concatenate([own, own], axis=1)

    def mix(dests):
        for dest in dests:
            part = acc[dest * 8 * blocks:(dest + 1) * 8 * blocks, :].reshape(blocks, 8, BLK)
            start = 8 * DEPTH + dest * 8 * blocks
            signal = xpad[start:start + 8 * blocks, :].reshape(blocks, 8, BLK)
            osend[dest] = (part + own[None] * signal).astype(bf16).reshape(8 * blocks, BLK)

    def send_mixed(first, count):
        def body(k, _):
            to = first + lax.rem(me + k, count)

            @pl.when(to != me)
            def _():
                mixed_copy(to, me).start()
            return 0

        lax.fori_loop(0, count, body, 0)

    answer(0, 0)

    def phase(p, _):
        lax.fori_loop(half * p, half * (p + 1), take_unit, 0)
        join_units(tiles, lower, half)

        @pl.when(p == 0)
        def _():
            @pl.when(early)
            def _():
                lax.fori_loop(half, n_unit, answer, 0)

            wait_blocks(1)
            wait_blocks(0)
            xpad[0:8 * DEPTH, :] = jnp.zeros((8 * DEPTH, BLK), f32)
            for source in range(n_ctx):
                for pair in range(2):
                    start = 8 * DEPTH + 8 * (source * blocks + 2 * pair)
                    xpad[start:start + 16, :] = xgot[pair, source].astype(f32)
            for q in range(DEPTH):
                xcat[:, BLK * q:BLK * (q + 1)] = xpad[8 * (DEPTH - q):8 * (DEPTH - q) + xcat.shape[0], :].astype(bf16)

        lower_half = early == (p == 0)

        @pl.when(lower_half)
        def _():
            half_conv(xcat, tiles, acc, 0, half * UNIT // 2)

        @pl.when(jnp.logical_not(lower_half))
        def _():
            half_conv(xcat, tiles, acc, 1, half * UNIT // 2)

        @pl.when(jnp.logical_and(early, p == 0))
        def _():
            mix(range(n_ctx // 2))
            send_mixed(0, n_ctx // 2)
        return 0

    lax.fori_loop(0, 2, phase, 0)

    @pl.when(early)
    def _():
        mix(range(n_ctx // 2, n_ctx))
        send_mixed(n_ctx // 2, n_ctx // 2)

    @pl.when(jnp.logical_not(early))
    def _():
        mix(range(n_ctx))
        send_mixed(0, n_ctx)

    ogot[me] = osend[me]

    def wait_mixed(k, _):
        mixed_copy(lax.rem(me + k, n_ctx), lax.rem(me + k, n_ctx)).wait_recv()
        return 0

    lax.fori_loop(1, n_ctx, wait_mixed, 0)

    wide = ogot[...].astype(f32)
    for i in range(blocks):
        piece = wide[:, 8 * i:8 * (i + 1), :].reshape(width, BLK).T
        rounded = qshort[BLK * i:BLK * (i + 1), :].astype(bf16).astype(f32)
        outv[BLK * i:BLK * (i + 1), :] = (rounded * piece).astype(bf16)
    store = pltpu.make_async_copy(outv, out_hbm, load_sem.at[0])
    store.start()

    @pl.when(me < n_ctx - 1)
    def _():
        for s in range(3):
            pltpu.make_async_remote_copy(raw.at[s, rows - 16:rows], halo.at[s], h_send.at[s], h_recv.at[s],
                                         device_id=(me + 1, ch), device_id_type=MESH).wait_send()

    def end_filter(k, _):
        filter_copy(lax.rem(ch + k, n_chan), ch).wait_send()
        return 0

    lax.fori_loop(1, n_chan, end_filter, 0)

    def end_blocks(k, _):
        to = lax.rem(me + k, n_ctx)
        block_copy(0, to, me).wait_send()
        block_copy(1, to, me).wait_send()
        mixed_copy(to, me).wait_send()
        return 0

    lax.fori_loop(1, n_ctx, end_blocks, 0)
    store.wait()


def local(mesh_shape, query_stream, key_stream, value_stream, short_weight, filter_rows, skip_weight):
    n_ctx, n_chan = mesh_shape
    rows, width = query_stream.shape
    piece = filter_rows.shape[1]
    total = rows * n_ctx // BLK * 8
    dma = pltpu.SemaphoreType.DMA
    return pl.pallas_call(
        functools.partial(kernel, n_ctx, n_chan),
        out_shape=jax.ShapeDtypeStruct((rows, width), bf16),
        in_specs=[pl.BlockSpec(memory_space=pltpu.HBM)] * 6,
        out_specs=pl.BlockSpec(memory_space=pl.ANY),
        scratch_shapes=[
            pltpu.VMEM((3, rows, width), bf16),
            pltpu.VMEM(short_weight.shape, f32),
            pltpu.VMEM((piece // LANE, filter_rows.shape[0], LANE), f32),
            pltpu.VMEM((1, width), f32),
            pltpu.VMEM((3, rows + 16, width), f32),
            pltpu.VMEM((3, 16, width), bf16),
            pltpu.VMEM((rows, width), f32),
            pltpu.VMEM((rows, width), f32),
            pltpu.VMEM((n_chan, piece // LANE, LANE), f32),
            pltpu.VMEM((n_chan, piece // LANE, LANE), f32),
            pltpu.VMEM((2, n_ctx, 16, BLK), bf16),
            pltpu.VMEM((2, n_ctx, 16, BLK), bf16),
            pltpu.VMEM((width, width), f32),
            pltpu.VMEM((total + 8 * DEPTH, BLK), f32),
            pltpu.VMEM((total, DEPTH * BLK), bf16),
            pltpu.VMEM((n_chan // 4 * UNIT + 3, LANE, LANE), bf16),
            pltpu.VMEM((n_chan // 4, LANE, LANE), bf16),
            pltpu.VMEM((total, BLK), f32),
            pltpu.VMEM((n_ctx, total // n_ctx, BLK), bf16),
            pltpu.VMEM((n_ctx, total // n_ctx, BLK), bf16),
            pltpu.VMEM((rows, width), bf16),
            dma((5 + piece // LANE,)),
            pltpu.SemaphoreType.REGULAR((n_chan,)),
            dma((3,)), dma((3,)),
            dma((n_chan,)), dma((n_chan,)),
            dma((2, n_ctx)), dma((2, n_ctx)),
            dma((n_ctx,)), dma((n_ctx,)),
        ],
        compiler_params=pltpu.CompilerParams(collective_id=0, has_side_effects=True, vmem_limit_bytes=63 * 1024 * 1024),
    )(query_stream, key_stream, value_stream, short_weight, filter_rows, skip_weight.reshape(1, width))


def solution(mesh):
    return jax.shard_map(
        functools.partial(local, (mesh.shape["ctx"], mesh.shape["chan"])),
        mesh=mesh,
        in_specs=(
            P("ctx", "chan"),
            P("ctx", "chan"),
            P("ctx", "chan"),
            P(None, None, "chan"),
            P(None, "chan"),
            P("chan"),
        ),
        out_specs=P("ctx", "chan"),
        check_vma=False,
    )
```

```python
import functools

import jax
import jax.numpy as jnp
from jax import lax
from jax.experimental import pallas as pl
from jax.experimental.pallas import tpu as pltpu
from jax.sharding import PartitionSpec as P

GROUP = 16
KSHORT = 7
BLK = 256
LANE = 128
MESH = pl.DeviceIdType.MESH
f32 = jnp.float32
bf16 = jnp.bfloat16


def short_rows(ext, taps, stream, start, count):
    total = taps[stream, 0:1, :] * ext[stream, 16 + start:16 + start + count, :]
    for j in range(1, KSHORT):
        total = total + taps[stream, j:j + 1, :] * ext[stream, 16 + start - j:16 + start - j + count, :]
    return total


UNIT = 8
DEPTH = 8


def unit_tiles(lines, tiles, lower, unit):
    row = lax.broadcasted_iota(jnp.int32, (LANE, LANE), 0)
    col = lax.broadcasted_iota(jnp.int32, (LANE, LANE), 1)
    keep = col >= row
    zero = jnp.zeros((LANE, LANE), f32)
    firsts = [pltpu.roll(jnp.broadcast_to(line, (8, LANE)), 0, 1, stride=1, stride_axis=0) for line in lines]
    before = zero
    for r in range(UNIT):
        now = jnp.concatenate([firsts[r]] + [pltpu.roll(firsts[r], 8 * k, 1) for k in range(1, LANE // 8)], axis=0)
        tiles[UNIT * unit + r + 1] = jnp.where(keep, now, before).astype(bf16)
        before = now
    lower[unit] = jnp.where(keep, zero, before).astype(bf16)


def join_units(tiles, lower, units):
    for unit in range(1, units):
        tiles[UNIT * unit + 1] = tiles[UNIT * unit + 1] + lower[unit - 1]
    tiles[UNIT * units + 1] = lower[units - 1]


def half_conv(xcat, tiles, acc, which, depths):
    total = xcat.shape[0]
    first = which * 8 * depths
    for e in range(depths // DEPTH):
        parts = []
        for q in range(DEPTH):
            d = e * DEPTH + q
            parts.append(jnp.concatenate([tiles[2 * d + 1], tiles[2 * d + 2]], axis=1))
            parts.append(jnp.concatenate([tiles[2 * d], tiles[2 * d + 1]], axis=1))
        start = first + 8 * DEPTH * e
        acc[start:total, :] += jnp.dot(xcat[0:total - start, :], jnp.concatenate(parts, axis=0), preferred_element_type=f32)
    start = first + 8 * depths
    if start < total:
        d = depths
        weights = jnp.concatenate([jnp.concatenate([tiles[2 * d + 1], tiles[2 * d + 2]], axis=1),
                                   jnp.concatenate([tiles[2 * d], tiles[2 * d + 1]], axis=1)], axis=0)
        acc[start:total, :] += jnp.dot(xcat[0:total - start, 0:BLK], weights, preferred_element_type=f32)


def kernel(n_ctx, n_chan, q_hbm, k_hbm, v_hbm, taps_hbm, filt_hbm, skip_hbm, out_hbm,
           raw, taps, filt, skip, ext, halo, qshort, prod, fsend, fgot, xsend, xgot, skipc, xpad, xcat, tiles, lower, acc,
           osend, ogot, outv,
           load_sem, ready, h_send, h_recv, f_send, f_recv, x_send, x_recv, o_send, o_recv):
    me = lax.axis_index("ctx")
    ch = lax.axis_index("chan")
    rows, width = raw.shape[1], raw.shape[2]
    blocks = rows // BLK

    streams = (q_hbm, k_hbm, v_hbm)
    loads = [pltpu.make_async_copy(streams[s], raw.at[s], load_sem.at[s]) for s in range(3)]
    loads.append(pltpu.make_async_copy(taps_hbm, taps, load_sem.at[3]))
    loads.append(pltpu.make_async_copy(skip_hbm, skip, load_sem.at[4]))
    pieces = filt.shape[0]
    for p in range(pieces):
        loads.append(pltpu.make_async_copy(filt_hbm.at[:, LANE * p:LANE * (p + 1)], filt.at[p], load_sem.at[5 + p]))
    for load in loads:
        load.start()

    barrier = pltpu.get_barrier_semaphore()

    core = lax.rem(me, 2)
    first = me - core

    def greet_ctx(k, _):
        to = lax.rem(me + k, n_ctx)

        @pl.when(lax.rem(to, 2) == 0)
        def _():
            pl.semaphore_signal(barrier, inc=1, device_id=(to, ch), device_id_type=MESH)
        return 0

    def greet_after(to, _):
        pl.semaphore_signal(barrier, inc=1, device_id=(first, to), device_id_type=MESH)
        return 0

    def greet_before(to, _):
        pl.semaphore_signal(barrier, inc=1, device_id=(first + 1, to), device_id_type=MESH)
        return 0

    lax.fori_loop(0, ch, greet_before, 0)
    lax.fori_loop(ch + 1, n_chan, greet_after, 0)
    lax.fori_loop(1, n_ctx, greet_ctx, 0)

    for load in loads:
        load.wait()

    for p in range(pieces):
        fsend[:, p, :] = filt[p, pl.ds(me // 2, n_chan, stride=8), :]

    def lay_out(pair):
        both = []
        for i in (2 * pair, 2 * pair + 1):
            both.append(prod[BLK * i:BLK * (i + 1), :].T.reshape(n_ctx, 8, BLK))
        xsend[pair] = jnp.concatenate(both, axis=1).astype(bf16)

    skipc[...] = jnp.broadcast_to(skip[...], (width, width)).T
    acc[...] = jnp.zeros_like(acc)
    tiles[0] = jnp.zeros((LANE, LANE), bf16)
    tiles[tiles.shape[0] - 1] = jnp.zeros((LANE, LANE), bf16)

    def filter_copy(to, side):
        return pltpu.make_async_remote_copy(fsend.at[to], fgot.at[ch], f_send.at[side, to], f_recv.at[ch],
                                            device_id=(first + side, to), device_id_type=MESH)

    def send_filter(to, _):
        for side in range(2):
            filter_copy(to, side).start()
        return 0

    @pl.when(core == 0)
    def _():
        pl.semaphore_wait(barrier, n_ctx - 1 + 2 * ch)
        pl.semaphore_signal(ready, inc=1, device_id=(me + 1, ch), device_id_type=MESH)
        lax.fori_loop(0, ch, send_filter, 0)

    @pl.when(core == 1)
    def _():
        pl.semaphore_wait(ready, 1)

    def send_after():
        @pl.when(ch < n_chan - 1)
        def _():
            pl.semaphore_wait(barrier, 2 * (n_chan - 1 - ch))
            lax.fori_loop(ch + 1, n_chan, send_filter, 0)

    fgot[ch] = fsend[ch]

    @pl.when(me < n_ctx - 1)
    def _():
        for s in range(3):
            pltpu.make_async_remote_copy(raw.at[s, rows - 16:rows], halo.at[s], h_send.at[s], h_recv.at[s],
                                         device_id=(me + 1, ch), device_id_type=MESH).start()

    def block_copy(pair, to, slot):
        return pltpu.make_async_remote_copy(xsend.at[pair, to], xgot.at[pair, slot], x_send.at[pair, to],
                                            x_recv.at[pair, slot], device_id=(to, ch), device_id_type=MESH)

    def send_blocks(pair):
        def body(k, _):
            block_copy(pair, lax.rem(me + k, n_ctx), me).start()
            return 0

        lax.fori_loop(1, n_ctx, body, 0)
        xgot[pair, me] = xsend[pair, me]

    for s in range(3):
        ext[s, 0:16, :] = jnp.zeros((16, width), f32)
        ext[s, 16:16 + rows, :] = raw[s].astype(f32)
    prod[...] = short_rows(ext, taps, 1, 0, rows) * short_rows(ext, taps, 2, 0, rows)
    lay_out(1)
    send_blocks(1)

    @pl.when(me > 0)
    def _():
        for s in range(3):
            pltpu.make_async_remote_copy(raw.at[s, rows - 16:rows], halo.at[s], h_send.at[s], h_recv.at[s],
                                         device_id=(me - 1, ch), device_id_type=MESH).wait_recv()
            ext[s, 0:16, :] = halo[s].astype(f32)
        prod[0:8, :] = short_rows(ext, taps, 1, 0, 8) * short_rows(ext, taps, 2, 0, 8)

    lay_out(0)
    send_blocks(0)
    qshort[...] = short_rows(ext, taps, 0, 0, rows)

    n_unit = n_chan // 2
    half = n_unit // 2
    mine = ch // 2
    place = lax.rem(mine, half)
    base = mine - place
    early = mine < half

    def unit_at(s):
        turn = jnp.where(s < half, s, n_unit - 1 - s)
        swing = jnp.where(turn % 2 == 1, place + (turn + 1) // 2, place - turn // 2)
        rest = jnp.where(place < half // 2, turn, half - 1 - turn)
        local_unit = jnp.where(turn <= 2 * jnp.minimum(place, half - 1 - place), swing, rest)
        return jnp.where(s < half, base, half - base) + local_unit

    def take_units(t, _):
        units = (unit_at(2 * t), unit_at(2 * t + 1))
        for unit in units:
            for y in range(2):
                source = 2 * unit + y

                @pl.when(source != ch)
                def _():
                    pltpu.make_async_remote_copy(fsend.at[0], fgot.at[source], f_send.at[0, 0], f_recv.at[source],
                                                 device_id=(me, source), device_id_type=MESH).wait_recv()

        lines = [[fgot[2 * unit + r // 4, r % 4:r % 4 + 1, :] for r in range(UNIT)] for unit in units]
        for unit, these in zip(units, lines):
            unit_tiles(these, tiles, lower, lax.rem(unit, half))
        return 0

    @pl.when(core == 1)
    def _():
        send_after()

    def wait_blocks(pair):
        def body(k, _):
            block_copy(pair, lax.rem(me + k, n_ctx), lax.rem(me + k, n_ctx)).wait_recv()
            return 0

        lax.fori_loop(1, n_ctx, body, 0)

    def mixed_copy(to, slot):
        return pltpu.make_async_remote_copy(osend.at[to], ogot.at[slot], o_send.at[to], o_recv.at[slot],
                                            device_id=(to, ch), device_id_type=MESH)

    own = skipc[pl.ds(pl.multiple_of(me * 8, 8), 8), :]
    own = jnp.concatenate([own, own], axis=1)

    def mix(dests):
        for dest in dests:
            part = acc[dest * 8 * blocks:(dest + 1) * 8 * blocks, :].reshape(blocks, 8, BLK)
            start = 8 * DEPTH + dest * 8 * blocks
            signal = xpad[start:start + 8 * blocks, :].reshape(blocks, 8, BLK)
            osend[dest] = (part + own[None] * signal).astype(bf16).reshape(8 * blocks, BLK)

    def send_mixed(first, count):
        def body(k, _):
            to = first + lax.rem(me + k, count)

            @pl.when(to != me)
            def _():
                mixed_copy(to, me).start()
            return 0

        lax.fori_loop(0, count, body, 0)

    def phase(p, _):
        lax.fori_loop(half // 2 * p, half // 2 * (p + 1), take_units, 0)
        join_units(tiles, lower, half)

        @pl.when(p == 0)
        def _():
            wait_blocks(1)
            wait_blocks(0)
            xpad[0:8 * DEPTH, :] = jnp.zeros((8 * DEPTH, BLK), f32)
            for source in range(n_ctx):
                for pair in range(2):
                    start = 8 * DEPTH + 8 * (source * blocks + 2 * pair)
                    xpad[start:start + 16, :] = xgot[pair, source].astype(f32)
            for q in range(DEPTH):
                xcat[:, BLK * q:BLK * (q + 1)] = xpad[8 * (DEPTH - q):8 * (DEPTH - q) + xcat.shape[0], :].astype(bf16)

        lower_half = early == (p == 0)

        @pl.when(lower_half)
        def _():
            half_conv(xcat, tiles, acc, 0, half * UNIT // 2)

        @pl.when(jnp.logical_not(lower_half))
        def _():
            half_conv(xcat, tiles, acc, 1, half * UNIT // 2)

        @pl.when(jnp.logical_and(early, p == 0))
        def _():
            mix(range(n_ctx // 2))
            send_mixed(0, n_ctx // 2)
        return 0

    lax.fori_loop(0, 2, phase, 0)

    @pl.when(early)
    def _():
        mix(range(n_ctx // 2, n_ctx))
        send_mixed(n_ctx // 2, n_ctx // 2)

    @pl.when(jnp.logical_not(early))
    def _():
        mix(range(n_ctx))
        send_mixed(0, n_ctx)

    ogot[me] = osend[me]

    def wait_mixed(k, _):
        mixed_copy(lax.rem(me + k, n_ctx), lax.rem(me + k, n_ctx)).wait_recv()
        return 0

    lax.fori_loop(1, n_ctx, wait_mixed, 0)

    wide = ogot[...].astype(f32)
    for i in range(blocks):
        piece = wide[:, 8 * i:8 * (i + 1), :].reshape(width, BLK).T
        rounded = qshort[BLK * i:BLK * (i + 1), :].astype(bf16).astype(f32)
        outv[BLK * i:BLK * (i + 1), :] = (rounded * piece).astype(bf16)
    store = pltpu.make_async_copy(outv, out_hbm, load_sem.at[0])
    store.start()

    @pl.when(me < n_ctx - 1)
    def _():
        for s in range(3):
            pltpu.make_async_remote_copy(raw.at[s, rows - 16:rows], halo.at[s], h_send.at[s], h_recv.at[s],
                                         device_id=(me + 1, ch), device_id_type=MESH).wait_send()

    def end_filter(to, _):
        for side in range(2):
            filter_copy(to, side).wait_send()
        return 0

    lax.fori_loop(jnp.where(core == 0, 0, ch + 1), jnp.where(core == 0, ch, n_chan), end_filter, 0)

    def end_blocks(k, _):
        to = lax.rem(me + k, n_ctx)
        block_copy(0, to, me).wait_send()
        block_copy(1, to, me).wait_send()
        mixed_copy(to, me).wait_send()
        return 0

    lax.fori_loop(1, n_ctx, end_blocks, 0)
    store.wait()


def local(mesh_shape, query_stream, key_stream, value_stream, short_weight, filter_rows, skip_weight):
    n_ctx, n_chan = mesh_shape
    rows, width = query_stream.shape
    piece = filter_rows.shape[1]
    total = rows * n_ctx // BLK * 8
    dma = pltpu.SemaphoreType.DMA
    return pl.pallas_call(
        functools.partial(kernel, n_ctx, n_chan),
        out_shape=jax.ShapeDtypeStruct((rows, width), bf16),
        in_specs=[pl.BlockSpec(memory_space=pltpu.HBM)] * 6,
        out_specs=pl.BlockSpec(memory_space=pl.ANY),
        scratch_shapes=[
            pltpu.VMEM((3, rows, width), bf16),
            pltpu.VMEM(short_weight.shape, f32),
            pltpu.VMEM((piece // LANE, filter_rows.shape[0], LANE), f32),
            pltpu.VMEM((1, width), f32),
            pltpu.VMEM((3, rows + 16, width), f32),
            pltpu.VMEM((3, 16, width), bf16),
            pltpu.VMEM((rows, width), f32),
            pltpu.VMEM((rows, width), f32),
            pltpu.VMEM((n_chan, piece // LANE, LANE), f32),
            pltpu.VMEM((n_chan, piece // LANE, LANE), f32),
            pltpu.VMEM((2, n_ctx, 16, BLK), bf16),
            pltpu.VMEM((2, n_ctx, 16, BLK), bf16),
            pltpu.VMEM((width, width), f32),
            pltpu.VMEM((total + 8 * DEPTH, BLK), f32),
            pltpu.VMEM((total, DEPTH * BLK), bf16),
            pltpu.VMEM((n_chan // 4 * UNIT + 3, LANE, LANE), bf16),
            pltpu.VMEM((n_chan // 4, LANE, LANE), bf16),
            pltpu.VMEM((total, BLK), f32),
            pltpu.VMEM((n_ctx, total // n_ctx, BLK), bf16),
            pltpu.VMEM((n_ctx, total // n_ctx, BLK), bf16),
            pltpu.VMEM((rows, width), bf16),
            dma((5 + piece // LANE,)),
            pltpu.SemaphoreType.REGULAR,
            dma((3,)), dma((3,)),
            dma((2, n_chan)), dma((n_chan,)),
            dma((2, n_ctx)), dma((2, n_ctx)),
            dma((n_ctx,)), dma((n_ctx,)),
        ],
        compiler_params=pltpu.CompilerParams(collective_id=0, has_side_effects=True, vmem_limit_bytes=63 * 1024 * 1024),
    )(query_stream, key_stream, value_stream, short_weight, filter_rows, skip_weight.reshape(1, width))


def solution(mesh):
    return jax.shard_map(
        functools.partial(local, (mesh.shape["ctx"], mesh.shape["chan"])),
        mesh=mesh,
        in_specs=(
            P("ctx", "chan"),
            P("ctx", "chan"),
            P("ctx", "chan"),
            P(None, None, "chan"),
            P(None, "chan"),
            P("chan"),
        ),
        out_specs=P("ctx", "chan"),
        check_vma=False,
    )
```
